32 devices in a mesh: row: 4 (over y, core), col: 8 (over z, x).
Axes of the slice: x: 2, y: 2, z: 4, core: 2. Of those that a mesh axis runs over, the one named last changes fastest.
Arguments:
- matrix: float32 [32768, 1024], P('row', 'col'), may hold values from -700 to 700, as said below
Outputs:
- r_rows: float32 [2, 128, 1024], P(None, None, 'col')
- factored: float32 [32768, 1024], P('row', 'col')
The draws below stay inside these ranges and needn't reach their ends.
Inputs may be any that keep to these rules, and one draw needn't show every extreme that they name: `matrix`: real-valued entries.
All inputs are finite; a program needn't handle non-finite values.
Results may differ from the reference program's by a relative error of at most 0.0003.
Values sent between devices are 32-bit elements; how exact they have to be, the bound alone decides.
A program may use at most 64 MiB of HBM per device.

```python
import math
import jax
import jax.numpy as jnp
from jax import lax

B = 128
ROWS = 32768
NCOL = 1024


def draw_matrix(key, part):
    keys = jax.random.split(key, 4)
    shared = jnp.clip(jax.random.normal(keys[0], (ROWS, B), jnp.float32), -4.0, 4.0)
    noise_part = jnp.clip(jax.random.normal(keys[1], (ROWS, NCOL), jnp.float32), -4.0, 4.0)
    row_spread = jnp.exp(jax.random.uniform(keys[3], (ROWS, 1), jnp.float32, 0.0, math.log(10.0)))
    weights = jnp.exp(jax.random.uniform(keys[2], (1, NCOL), jnp.float32, math.log(0.5), math.log(2.0)))
    tiled = jnp.tile(shared, (1, NCOL // B))
    row_ids = jnp.arange(ROWS, dtype=jnp.int32)[:, None]
    col_ids = jnp.arange(NCOL, dtype=jnp.int32)[None, :]
    planted = jnp.where((row_ids + 37 * (col_ids // B)) % B == col_ids % B, 2.0, 0.0).astype(jnp.float32)
    ramp = 1.0 + 2.0 * jnp.arange(ROWS, dtype=jnp.float32)[:, None] / (ROWS - 1)
    return (row_spread * ramp * (weights * tiled + noise_part + planted)).astype(jnp.float32)


def setup_inputs(seed: int = 0) -> dict:
    splits = jax.random.split(jax.random.key(seed), 2)
    matrix = draw_matrix(jax.random.fold_in(splits[1], 71), 0)
    return dict(matrix=matrix)


def gram_matrix(block):
    return lax.dot_general(block, block, (((0,), (0,)), ((), ())), precision=lax.Precision.HIGHEST)

def reference(matrix):
    factor_scale = math.sqrt(ROWS)
    working = matrix
    couplings = []
    first_basis = None
    for panel_id in range(2):
        panel_rows = working[:, panel_id * B:(panel_id + 1) * B]
        lower_factor = jnp.linalg.cholesky(gram_matrix(panel_rows))
        inverse_lower = jax.scipy.linalg.solve_triangular(lower_factor, jnp.eye(B, dtype=jnp.float32), lower=True)
        basis_rows = lax.dot_general(panel_rows, inverse_lower, (((1,), (1,)), ((), ())), precision=lax.Precision.HIGHEST)
        cross_rows = lax.dot_general(basis_rows, working, (((0,), (0,)), ((), ())), precision=lax.Precision.HIGHEST)
        working = working - jnp.dot(basis_rows, cross_rows, precision=lax.Precision.HIGHEST)
        scaled_basis = factor_scale * basis_rows
        working = working.at[:, panel_id * B:(panel_id + 1) * B].set(scaled_basis)
        if panel_id == 0:
            first_basis = scaled_basis
        couplings.append(cross_rows / factor_scale)
    working = working.at[:, 0:B].set(first_basis)
    return (jnp.stack(couplings), working)
```

```python
import functools
import math

import jax
import jax.numpy as jnp
from jax import lax
from jax.experimental import pallas as pl
from jax.experimental.pallas import tpu as pltpu
from jax.sharding import PartitionSpec as P

MESH = pl.DeviceIdType.MESH
HIGHEST = lax.Precision.HIGHEST
PANELS = 2
LAG = 3


def outer(a, b):
    return lax.dot_general(
        a, b, (((0,), (0,)), ((), ())), precision=HIGHEST, preferred_element_type=jnp.float32
    )


def gather_kernel(
    n_row, n_x, n_z, tile,
    matrix_ref, panels_out, sums_out,
    panels, mine, sums, parts, total,
    mine_sem, recv_sem, send_sem, out_sem, rs_send, rs_recv, ag_send, ag_recv,
):
    rows, width = mine.shape
    steps = rows // tile
    row = lax.axis_index("row")
    col = lax.axis_index("col")
    x = lax.rem(col, n_x)
    z = col // n_x

    barrier = pltpu.get_barrier_semaphore()
    neighbours = (
        (x > 0, col - 1), (x < n_x - 1, col + 1), (z > 0, col - n_x), (z < n_z - 1, col + n_x)
    )
    for there, other in neighbours:
        @pl.when(there)
        def _():
            pl.semaphore_signal(barrier, inc=1, device_id={"col": other}, device_id_type=MESH)
    for step in range(1, n_row):
        peer = lax.rem(row + step, n_row)
        pl.semaphore_signal(barrier, inc=1, device_id={"row": peer}, device_id_type=MESH)
    load_mine = pltpu.make_async_copy(matrix_ref, mine, mine_sem)
    load_mine.start()
    peers = n_row - 1
    for there, _ in neighbours:
        peers += jnp.where(there, 1, 0)
    pl.semaphore_wait(barrier, peers)

    def span(index):
        return pl.ds(pl.multiple_of(index * tile, tile), tile)

    def children(panel):
        return (
            (jnp.logical_and(x == panel, z < n_z - 1), col + n_x),
            (jnp.logical_and(x >= panel, x < n_x - 1), col + 1),
            (jnp.logical_and(x <= panel, x > 0), col - 1),
        )

    def forward(panel, index, source):
        for child, (there, other) in enumerate(children(panel)):
            @pl.when(there)
            def _():
                pltpu.make_async_remote_copy(
                    src_ref=source.at[span(index)],
                    dst_ref=panels.at[panel, span(index)],
                    send_sem=send_sem.at[panel, child],
                    recv_sem=recv_sem.at[panel, index],
                    device_id={"col": other},
                    device_id_type=MESH,
                ).start()

    owner = col < PANELS

    @pl.when(owner)
    def _():
        @pl.loop(0, steps)
        def _(index):
            forward(col, index, matrix_ref)
            pltpu.make_async_copy(
                matrix_ref.at[span(index)], panels.at[col, span(index)], recv_sem.at[col, index]
            ).start()

    main = jnp.where(x == 1, 1, 0)
    second = 1 - main

    def take(panel, index):
        pltpu.make_async_copy(
            matrix_ref.at[span(index)], panels.at[panel, span(index)], recv_sem.at[panel, index]
        ).wait()

        @pl.when(col != panel)
        def _():
            forward(panel, index, panels.at[panel])

        pltpu.make_async_copy(
            panels.at[panel, span(index)], panels_out.at[panel, span(index)], out_sem.at[panel]
        ).start()

    sums[...] = jnp.zeros_like(sums)
    load_mine.wait()

    @pl.loop(0, steps + LAG)
    def _(step):
        @pl.when(step < steps)
        def _():
            take(main, step)

        @pl.when(step >= LAG)
        def _():
            index = step - LAG
            take(second, index)
            first = panels[0, span(index)]
            other = panels[1, span(index)]
            both = jnp.concatenate([first, other], axis=1)
            right = jnp.concatenate([first, other, mine[span(index)]], axis=1)
            sums[...] += outer(both, right)

    share = sums.shape[0] // n_row

    def part(index):
        return pl.ds(pl.multiple_of(index * share, share), share)

    scatters = []
    for step in range(1, n_row):
        peer = lax.rem(row + step, n_row)
        copy = pltpu.make_async_remote_copy(
            src_ref=sums.at[part(peer)],
            dst_ref=parts.at[step - 1],
            send_sem=rs_send.at[step - 1],
            recv_sem=rs_recv.at[step - 1],
            device_id={"row": peer},
            device_id_type=MESH,
        )
        copy.start()
        scatters.append(copy)
    summed = sums[part(row)]
    for step, copy in enumerate(scatters):
        copy.wait_recv()
        summed += parts[step]
    total[part(row)] = summed
    gathers = []
    for step in range(1, n_row):
        peer = lax.rem(row + step, n_row)
        copy = pltpu.make_async_remote_copy(
            src_ref=total.at[part(row)],
            dst_ref=total.at[part(row)],
            send_sem=ag_send.at[step - 1],
            recv_sem=ag_recv.at[step - 1],
            device_id={"row": peer},
            device_id_type=MESH,
        )
        copy.start()
        gathers.append(copy)
    for copy in gathers:
        copy.wait_recv()
    sums_out[...] = total[...]

    for copy in scatters + gathers:
        copy.wait_send()
    for panel in range(PANELS):
        pltpu.make_async_copy(panels.at[panel], panels_out.at[panel], out_sem.at[panel]).wait()
        for child, (there, other) in enumerate(children(panel)):
            @pl.when(there)
            def _():
                pltpu.make_async_remote_copy(
                    src_ref=panels.at[panel],
                    dst_ref=panels.at[panel],
                    send_sem=send_sem.at[panel, child],
                    recv_sem=recv_sem.at[panel, 0],
                    device_id={"col": other},
                    device_id_type=MESH,
                ).wait_send()


def gather(matrix, n_row, n_x, n_z):
    rows, width = matrix.shape
    tile = math.gcd(rows, 256)
    steps = rows // tile
    deep, wide = PANELS * width, (PANELS + 1) * width
    share = deep // n_row
    anywhere = pl.BlockSpec(memory_space=pl.ANY)
    return pl.pallas_call(
        functools.partial(gather_kernel, n_row, n_x, n_z, tile),
        out_shape=(
            jax.ShapeDtypeStruct((PANELS, rows, width), jnp.float32),
            jax.ShapeDtypeStruct((deep, wide), jnp.float32),
        ),
        in_specs=[anywhere],
        out_specs=(anywhere, pl.BlockSpec(memory_space=pltpu.VMEM)),
        scratch_shapes=[
            pltpu.VMEM((PANELS, rows, width), jnp.float32),
            pltpu.VMEM((rows, width), jnp.float32),
            pltpu.VMEM((deep, wide), jnp.float32),
            pltpu.VMEM((n_row - 1, share, wide), jnp.float32),
            pltpu.VMEM((deep, wide), jnp.float32),
            pltpu.SemaphoreType.DMA,
            pltpu.SemaphoreType.DMA((PANELS, steps)),
            pltpu.SemaphoreType.DMA((PANELS, 3)),
            pltpu.SemaphoreType.DMA((PANELS,)),
            pltpu.SemaphoreType.DMA((n_row - 1,)),
            pltpu.SemaphoreType.DMA((n_row - 1,)),
            pltpu.SemaphoreType.DMA((n_row - 1,)),
            pltpu.SemaphoreType.DMA((n_row - 1,)),
        ],
        compiler_params=pltpu.CompilerParams(
            collective_id=0, has_side_effects=True, vmem_limit_bytes=60 * 1024 * 1024
        ),
    )(matrix)


def update_kernel(panels_ref, matrix_ref, mix_ref, out_ref):
    width = matrix_ref.shape[1]
    keep = lax.axis_index("col") >= PANELS
    product = jnp.dot(panels_ref[0], mix_ref[:width], precision=HIGHEST)
    product += jnp.dot(panels_ref[1], mix_ref[width:], precision=HIGHEST)
    out_ref[...] = jnp.where(keep, matrix_ref[...], 0.0) - product


def update(panels, matrix, mix):
    rows, width = matrix.shape
    tile = math.gcd(rows, 1024)
    return pl.pallas_call(
        update_kernel,
        grid=(rows // tile,),
        out_shape=jax.ShapeDtypeStruct((rows, width), jnp.float32),
        in_specs=[
            pl.BlockSpec((PANELS, tile, width), lambda i: (0, i, 0)),
            pl.BlockSpec((tile, width), lambda i: (i, 0)),
            pl.BlockSpec((PANELS * width, width), lambda i: (0, 0)),
        ],
        out_specs=pl.BlockSpec((tile, width), lambda i: (i, 0)),
        compiler_params=pltpu.CompilerParams(vmem_limit_bytes=40 * 1024 * 1024),
    )(panels, matrix, mix)


def product(a, b):
    return jnp.dot(a, b, precision=HIGHEST)


def inverse_of(lower_factor):
    width = lower_factor.shape[0]
    return jax.scipy.linalg.solve_triangular(
        lower_factor, jnp.eye(width, dtype=jnp.float32), lower=True
    )


def coefficients(sums, factor_scale, width):
    col = lax.axis_index("col")
    g00, g01 = sums[:width, :width], sums[:width, width:2 * width]
    g11 = sums[width:, width:2 * width]
    m0, m1 = sums[:width, 2 * width:], sums[width:, 2 * width:]
    scaled_eye = factor_scale * jnp.eye(width, dtype=jnp.float32)
    inv0 = inverse_of(jnp.linalg.cholesky(g00))
    both = product(inv0, jnp.concatenate([m0, g01], axis=1))
    cross0, r01 = both[:, :width], both[:, width:]
    lower1 = jnp.linalg.cholesky(g11 - product(r01.T, r01))
    inv1 = inverse_of(lower1)
    scaled = factor_scale * product(jnp.concatenate([g00, g01.T], axis=0), inv0.T)
    n0 = jnp.where(col == 0, scaled[:width], m0)
    n1 = jnp.where(col == 0, scaled[width:], m1)
    cross1 = product(inv1, n1 - product(r01.T, product(inv0, n0)))
    t1 = jnp.where(col == 1, -scaled_eye, jnp.where(col == 0, 0.0, cross1))
    t0 = jnp.where(col == 0, -scaled_eye, jnp.where(col == 1, 0.0, cross0))
    x1 = product(inv1.T, t1)
    x0 = product(inv0.T, t0 - product(r01, x1))
    return jnp.stack([cross0, cross1]) / factor_scale, jnp.concatenate([x0, x1], axis=0)


def solution(mesh):
    n_row, n_col = mesh.shape["row"], mesh.shape["col"]
    n_x = max(PANELS, n_row // 2)
    n_z = n_col // n_x
    assert n_x * n_z == n_col

    def local(matrix):
        rows, width = matrix.shape
        factor_scale = math.sqrt(rows * n_row)
        panels, sums = gather(matrix, n_row, n_x, n_z)
        r_rows, mix = coefficients(sums, factor_scale, width)
        return r_rows, update(panels, matrix, mix)

    return jax.shard_map(
        local,
        mesh=mesh,
        in_specs=(P("row", "col"),),
        out_specs=(P(None, None, "col"), P("row", "col")),
        check_vma=False,
    )
```

```python
import functools
import math

import jax
import jax.numpy as jnp
from jax import lax
from jax.experimental import pallas as pl
from jax.experimental.pallas import tpu as pltpu
from jax.sharding import PartitionSpec as P

MESH = pl.DeviceIdType.MESH
HIGHEST = lax.Precision.HIGHEST
PANELS = 2
LAG = 4
BLOCK = 32


def outer(a, b):
    return lax.dot_general(
        a, b, (((0,), (0,)), ((), ())), precision=HIGHEST, preferred_element_type=jnp.float32
    )


def gather_kernel(
    n_row, n_x, n_z, tile,
    matrix_ref, panels_out, sums_out,
    panels, mine, sums, parts, total,
    mine_sem, recv_sem, send_sem, out_sem, rs_send, rs_recv, ag_send, ag_recv,
):
    rows, width = mine.shape
    steps = rows // tile
    row = lax.axis_index("row")
    col = lax.axis_index("col")
    x = lax.rem(col, n_x)
    z = col // n_x

    barrier = pltpu.get_barrier_semaphore()
    neighbours = (
        (x > 0, col - 1), (x < n_x - 1, col + 1), (z > 0, col - n_x), (z < n_z - 1, col + n_x)
    )
    for there, other in neighbours:
        @pl.when(there)
        def _():
            pl.semaphore_signal(barrier, inc=1, device_id={"col": other}, device_id_type=MESH)
    for step in range(1, n_row):
        peer = lax.rem(row + step, n_row)
        pl.semaphore_signal(barrier, inc=1, device_id={"row": peer}, device_id_type=MESH)
    load_mine = pltpu.make_async_copy(matrix_ref, mine, mine_sem)
    load_mine.start()
    peers = n_row - 1
    for there, _ in neighbours:
        peers += jnp.where(there, 1, 0)
    pl.semaphore_wait(barrier, peers)

    def span(index):
        return pl.ds(pl.multiple_of(index * tile, tile), tile)

    def children(panel):
        return (
            (jnp.logical_and(x == panel, z < n_z - 1), col + n_x),
            (jnp.logical_and(x >= panel, x < n_x - 1), col + 1),
            (jnp.logical_and(x <= panel, x > 0), col - 1),
        )

    def forward(panel, index, source):
        for child, (there, other) in enumerate(children(panel)):
            @pl.when(there)
            def _():
                pltpu.make_async_remote_copy(
                    src_ref=source.at[span(index)],
                    dst_ref=panels.at[panel, span(index)],
                    send_sem=send_sem.at[panel, child],
                    recv_sem=recv_sem.at[panel, index],
                    device_id={"col": other},
                    device_id_type=MESH,
                ).start()

    owner = col < PANELS

    @pl.when(owner)
    def _():
        @pl.loop(0, steps)
        def _(index):
            forward(col, index, matrix_ref)
            pltpu.make_async_copy(
                matrix_ref.at[span(index)], panels.at[col, span(index)], recv_sem.at[col, index]
            ).start()

    main = jnp.where(x == 1, 1, 0)
    second = 1 - main

    def take(panel, index):
        pltpu.make_async_copy(
            matrix_ref.at[span(index)], panels.at[panel, span(index)], recv_sem.at[panel, index]
        ).wait()

        @pl.when(col != panel)
        def _():
            forward(panel, index, panels.at[panel])

        pltpu.make_async_copy(
            panels.at[panel, span(index)], panels_out.at[panel, span(index)], out_sem.at[panel]
        ).start()

    sums[...] = jnp.zeros_like(sums)
    load_mine.wait()

    @pl.loop(0, steps + LAG)
    def _(step):
        @pl.when(step < steps)
        def _():
            take(main, step)

        @pl.when(step >= LAG)
        def _():
            index = step - LAG
            take(second, index)
            first = panels[0, span(index)]
            other = panels[1, span(index)]
            both = jnp.concatenate([first, other], axis=1)
            right = jnp.concatenate([first, other, mine[span(index)]], axis=1)
            sums[...] += outer(both, right)

    share = sums.shape[0] // n_row

    def part(index):
        return pl.ds(pl.multiple_of(index * share, share), share)

    scatters = []
    for step in range(1, n_row):
        peer = lax.rem(row + step, n_row)
        copy = pltpu.make_async_remote_copy(
            src_ref=sums.at[part(peer)],
            dst_ref=parts.at[step - 1],
            send_sem=rs_send.at[step - 1],
            recv_sem=rs_recv.at[step - 1],
            device_id={"row": peer},
            device_id_type=MESH,
        )
        copy.start()
        scatters.append(copy)
    summed = sums[part(row)]
    for step, copy in enumerate(scatters):
        copy.wait_recv()
        summed += parts[step]
    total[part(row)] = summed
    gathers = []
    for step in range(1, n_row):
        peer = lax.rem(row + step, n_row)
        copy = pltpu.make_async_remote_copy(
            src_ref=total.at[part(row)],
            dst_ref=total.at[part(row)],
            send_sem=ag_send.at[step - 1],
            recv_sem=ag_recv.at[step - 1],
            device_id={"row": peer},
            device_id_type=MESH,
        )
        copy.start()
        gathers.append(copy)
    for copy in gathers:
        copy.wait_recv()
    sums_out[...] = total[...]

    for copy in scatters + gathers:
        copy.wait_send()
    for panel in range(PANELS):
        pltpu.make_async_copy(panels.at[panel], panels_out.at[panel], out_sem.at[panel]).wait()
        for child, (there, other) in enumerate(children(panel)):
            @pl.when(there)
            def _():
                pltpu.make_async_remote_copy(
                    src_ref=panels.at[panel],
                    dst_ref=panels.at[panel],
                    send_sem=send_sem.at[panel, child],
                    recv_sem=recv_sem.at[panel, 0],
                    device_id={"col": other},
                    device_id_type=MESH,
                ).wait_send()


def gather(matrix, n_row, n_x, n_z):
    rows, width = matrix.shape
    tile = math.gcd(rows, 128)
    steps = rows // tile
    deep, wide = PANELS * width, (PANELS + 1) * width
    share = deep // n_row
    anywhere = pl.BlockSpec(memory_space=pl.ANY)
    return pl.pallas_call(
        functools.partial(gather_kernel, n_row, n_x, n_z, tile),
        out_shape=(
            jax.ShapeDtypeStruct((PANELS, rows, width), jnp.float32),
            jax.ShapeDtypeStruct((deep, wide), jnp.float32),
        ),
        in_specs=[anywhere],
        out_specs=(anywhere, pl.BlockSpec(memory_space=pltpu.VMEM)),
        scratch_shapes=[
            pltpu.VMEM((PANELS, rows, width), jnp.float32),
            pltpu.VMEM((rows, width), jnp.float32),
            pltpu.VMEM((deep, wide), jnp.float32),
            pltpu.VMEM((n_row - 1, share, wide), jnp.float32),
            pltpu.VMEM((deep, wide), jnp.float32),
            pltpu.SemaphoreType.DMA,
            pltpu.SemaphoreType.DMA((PANELS, steps)),
            pltpu.SemaphoreType.DMA((PANELS, 3)),
            pltpu.SemaphoreType.DMA((PANELS,)),
            pltpu.SemaphoreType.DMA((n_row - 1,)),
            pltpu.SemaphoreType.DMA((n_row - 1,)),
            pltpu.SemaphoreType.DMA((n_row - 1,)),
            pltpu.SemaphoreType.DMA((n_row - 1,)),
        ],
        compiler_params=pltpu.CompilerParams(
            collective_id=0, has_side_effects=True, vmem_limit_bytes=60 * 1024 * 1024
        ),
    )(matrix)


def product(a, b, over=((1,), (0,))):
    return lax.dot_general(
        a, b, (over, ((), ())), precision=HIGHEST, preferred_element_type=jnp.float32
    )


def inverse_factor(gram):
    width = gram.shape[0]
    left, right = gram, eye(width)
    row_id = lax.broadcasted_iota(jnp.int32, (BLOCK, 1), 0)
    lane = lax.broadcasted_iota(jnp.int32, (BLOCK, width), 1)
    done = []
    for start in range(0, width, BLOCK):
        p, e = left[:BLOCK], right[:BLOCK]
        for s in range(BLOCK):
            column = p[:, start + s:start + s + 1]
            ratio = jnp.where(row_id > s, column / column[s:s + 1], 0.0)
            p, e = p - ratio * p[s:s + 1], e - ratio * e[s:s + 1]
        pivots = jnp.sum(jnp.where(lane == row_id + start, p, 0.0), axis=1, keepdims=True)
        scale = 1.0 / jnp.sqrt(pivots)
        p, e = p * scale, e * scale
        done.append(e)
        if start + BLOCK < width:
            change = outer(p, jnp.concatenate([p, e], axis=1))
            left = left[BLOCK:] - change[start + BLOCK:, :width]
            right = right[BLOCK:] - change[start + BLOCK:, width:]
    return jnp.concatenate(done, axis=0)


def eye(width):
    rows = lax.broadcasted_iota(jnp.int32, (width, width), 0)
    return jnp.where(rows == lax.broadcasted_iota(jnp.int32, (width, width), 1), 1.0, 0.0)


def coefficients(sums, factor_scale, width, col):
    g00, g01 = sums[:width, :width], sums[:width, width:2 * width]
    g10, g11 = sums[width:, :width], sums[width:, width:2 * width]
    m0, m1 = sums[:width, 2 * width:], sums[width:, 2 * width:]
    scaled_eye = factor_scale * eye(width)
    down, turned = ((0,), (0,)), ((1,), (1,))
    inv0 = inverse_factor(g00)
    both = product(inv0, jnp.concatenate([m0, g01], axis=1))
    cross0, r01 = both[:, :width], both[:, width:]
    inv1 = inverse_factor(g11 - product(r01, r01, down))
    n0 = jnp.where(col == 0, factor_scale * product(g00, inv0, turned), m0)
    n1 = jnp.where(col == 0, factor_scale * product(g10, inv0, turned), m1)
    cross1 = product(inv1, n1 - product(r01, product(inv0, n0), down))
    t1 = jnp.where(col == 1, -scaled_eye, jnp.where(col == 0, 0.0, cross1))
    t0 = jnp.where(col == 0, -scaled_eye, jnp.where(col == 1, 0.0, cross0))
    x1 = product(inv1, t1, down)
    x0 = product(inv0, t0 - product(r01, x1), down)
    return cross0, cross1, jnp.concatenate([x0, x1], axis=0)


def halves(a):
    high = a.astype(jnp.bfloat16)
    return high, (a - high.astype(jnp.float32)).astype(jnp.bfloat16)


def finish_kernel(
    factor_scale, tile, panels_ref, matrix_ref, sums_ref, r_ref, out_ref,
    panels, mine, result, load_sem, out_sem,
):
    rows, width = mine.shape
    load_panels = pltpu.make_async_copy(panels_ref, panels, load_sem.at[0])
    load_mine = pltpu.make_async_copy(matrix_ref, mine, load_sem.at[1])
    load_panels.start()
    load_mine.start()
    col = lax.axis_index("col")
    cross0, cross1, mix = coefficients(sums_ref[...], factor_scale, width, col)
    r_ref[0] = cross0 / factor_scale
    r_ref[1] = cross1 / factor_scale
    mix_high, mix_low = halves(mix)
    mix_both = jnp.concatenate([mix_high, mix_low], axis=1)
    load_panels.wait()
    load_mine.wait()
    keep = col >= PANELS

    @pl.loop(0, rows // tile)
    def _(index):
        at = pl.ds(pl.multiple_of(index * tile, tile), tile)
        high, low = halves(jnp.concatenate([panels[0, at], panels[1, at]], axis=1))
        main = jnp.dot(high, mix_both, preferred_element_type=jnp.float32)
        rest = jnp.dot(low, mix_high, preferred_element_type=jnp.float32)
        removed = main[:, :width] + (main[:, width:] + rest)
        result[at] = jnp.where(keep, mine[at], 0.0) - removed
        pltpu.make_async_copy(result.at[at], out_ref.at[at], out_sem).start()

    pltpu.make_async_copy(result, out_ref, out_sem).wait()


def finish(panels, matrix, sums, factor_scale):
    rows, width = matrix.shape
    anywhere = pl.BlockSpec(memory_space=pl.ANY)
    in_vmem = pl.BlockSpec(memory_space=pltpu.VMEM)
    return pl.pallas_call(
        functools.partial(finish_kernel, factor_scale, math.gcd(rows, 512)),
        out_shape=(
            jax.ShapeDtypeStruct((PANELS, width, width), jnp.float32),
            jax.ShapeDtypeStruct((rows, width), jnp.float32),
        ),
        in_specs=[anywhere, anywhere, in_vmem],
        out_specs=(in_vmem, anywhere),
        scratch_shapes=[
            pltpu.VMEM((PANELS, rows, width), jnp.float32),
            pltpu.VMEM((rows, width), jnp.float32),
            pltpu.VMEM((rows, width), jnp.float32),
            pltpu.SemaphoreType.DMA((2,)),
            pltpu.SemaphoreType.DMA,
        ],
        compiler_params=pltpu.CompilerParams(vmem_limit_bytes=60 * 1024 * 1024),
    )(panels, matrix, sums)


def solution(mesh):
    n_row, n_col = mesh.shape["row"], mesh.shape["col"]
    n_x = max(PANELS, n_row // 2)
    n_z = n_col // n_x
    assert n_x * n_z == n_col

    def local(matrix):
        rows, width = matrix.shape
        factor_scale = math.sqrt(rows * n_row)
        panels, sums = gather(matrix, n_row, n_x, n_z)
        return finish(panels, matrix, sums, factor_scale)

    return jax.shard_map(
        local,
        mesh=mesh,
        in_specs=(P("row", "col"),),
        out_specs=(P(None, None, "col"), P("row", "col")),
        check_vma=False,
    )
```

```python
import functools
import math

import jax
import jax.numpy as jnp
from jax import lax
from jax.experimental import pallas as pl
from jax.experimental.pallas import tpu as pltpu
from jax.sharding import PartitionSpec as P

MESH = pl.DeviceIdType.MESH
HIGHEST = lax.Precision.HIGHEST
PANELS = 2
LAG = 4
BLOCK = 32
EXTRA = 2
AHEAD = 6


def outer(a, b):
    return lax.dot_general(
        a, b, (((0,), (0,)), ((), ())), precision=HIGHEST, preferred_element_type=jnp.float32
    )


def gather_kernel(
    n_row, n_x, n_z, tile,
    matrix_ref, panels_out, sums_out,
    panels, mine, mixed, half, theirs, parts, total,
    mine_sem, recv_sem, send_sem, out_sem, scatter_send, scatter_recv, back_send, back_recv,
    swap_sem,
):
    rows, width = mine.shape
    steps = rows // tile
    row = lax.axis_index("row")
    col = lax.axis_index("col")
    x = lax.rem(col, n_x)
    z = col // n_x

    barrier = pltpu.get_barrier_semaphore()
    neighbours = (
        (x > 0, col - 1), (x < n_x - 1, col + 1), (z > 0, col - n_x), (z < n_z - 1, col + n_x)
    )
    for there, other in neighbours:
        @pl.when(there)
        def _():
            pl.semaphore_signal(barrier, inc=1, device_id={"col": other}, device_id_type=MESH)
    for step in range(1, n_row):
        peer = lax.rem(row + step, n_row)
        pl.semaphore_signal(barrier, inc=1, device_id={"row": peer}, device_id_type=MESH)
    load_mine = pltpu.make_async_copy(matrix_ref, mine, mine_sem)
    load_mine.start()
    mixed[...] = jnp.zeros_like(mixed)
    peers = n_row - 1
    for there, _ in neighbours:
        peers += jnp.where(there, 1, 0)
    pl.semaphore_wait(barrier, peers)

    def span(panel, index):
        turned = jnp.logical_and(panel == 1, index < steps)
        place = jnp.where(turned, steps - 1 - index, index)
        return pl.ds(pl.multiple_of(place * tile, tile), tile)

    def children(panel):
        return (
            (jnp.logical_and(x == panel, z < n_z - 1), col + n_x),
            (jnp.logical_and(x >= panel, x < n_x - 1), col + 1),
            (jnp.logical_and(x <= panel, x > 0), col - 1),
        )

    def forward(panel, index, source, which=(0, 1, 2)):
        for child, (there, other) in enumerate(children(panel)):
            if child not in which:
                continue

            @pl.when(there)
            def _():
                pltpu.make_async_remote_copy(
                    src_ref=source.at[span(panel, index)],
                    dst_ref=panels.at[panel, span(panel, index)],
                    send_sem=send_sem.at[panel, child],
                    recv_sem=recv_sem.at[panel, index],
                    device_id={"col": other},
                    device_id_type=MESH,
                ).start()

    def keep(panel, index):
        pltpu.make_async_copy(
            panels.at[panel, span(panel, index)],
            panels_out.at[panel, span(panel, index)],
            out_sem.at[panel],
        ).start()

    def take(panel, index):
        here = panels.at[panel, span(panel, index)]
        pltpu.make_async_copy(here, here, recv_sem.at[panel, index]).wait()
        forward(panel, index, panels.at[panel])
        keep(panel, index)

    def add(panel, index, source):
        at = span(panel, index)
        block = pl.ds(pl.multiple_of(panel * width, width), width)
        mixed[block] += outer(source[at], mine[at])

    share = mixed.shape[0] // n_row

    def part(index):
        return pl.ds(pl.multiple_of(index * share, share), share)

    def sum_over_row(source, turn):
        copies = []
        for step in range(1, n_row):
            peer = lax.rem(row + step, n_row)
            copies.append(pltpu.make_async_remote_copy(
                src_ref=source.at[part(peer)],
                dst_ref=parts.at[turn, step - 1],
                send_sem=scatter_send.at[turn, step - 1],
                recv_sem=scatter_recv.at[turn, step - 1],
                device_id={"row": peer},
                device_id_type=MESH,
            ))
            copies[-1].start()
        summed = source[part(row)]
        for step, copy in enumerate(copies):
            copy.wait_recv()
            summed += parts[turn, step]
        result = total.at[turn]
        result[part(row)] = summed
        backs = []
        for step in range(1, n_row):
            peer = lax.rem(row + step, n_row)
            backs.append(pltpu.make_async_remote_copy(
                src_ref=result.at[part(row)],
                dst_ref=result.at[part(row)],
                send_sem=back_send.at[turn, step - 1],
                recv_sem=back_recv.at[turn, step - 1],
                device_id={"row": peer},
                device_id_type=MESH,
            ))
            backs[-1].start()
        for copy in backs:
            copy.wait_recv()
        for copy in copies + backs:
            copy.wait_send()

    main = jnp.where(x == 1, 1, 0)
    second = 1 - main
    owner = col < PANELS
    middle = steps // 2
    load_mine.wait()

    @pl.when(owner)
    def _():
        @pl.loop(0, middle + AHEAD)
        def _(index):
            forward(col, index, matrix_ref)

        @pl.loop(middle + AHEAD, steps)
        def _(index):
            forward(col, index, matrix_ref, (0,))

        own = pltpu.make_async_copy(
            mine, panels_out.at[col, pl.ds(0, rows)], out_sem.at[col]
        )
        own.start()

        @pl.loop(0, steps)
        def _(index):
            add(col, index, mine)

        @pl.loop(0, middle)
        def _(index):
            take(second, index)
            add(second, index, panels.at[second])

        half[...] = mixed[...]
        sum_over_row(half, 0)
        swap = pltpu.make_async_remote_copy(
            src_ref=total.at[0],
            dst_ref=theirs,
            send_sem=swap_sem.at[0],
            recv_sem=swap_sem.at[1],
            device_id={"col": 1 - col},
            device_id_type=MESH,
        )
        swap.start()

        @pl.loop(middle + AHEAD, steps)
        def _(index):
            forward(col, index, matrix_ref, (1, 2))

        swap.wait()
        first = col == 0
        ours, other = total[0], theirs[...]
        left = jnp.where(first, ours, other)
        right = jnp.where(first, other, ours)
        inv0 = inverse_factor(left[:width])
        r01 = product(inv0, right[:width]) + product(inv0, left[width:], ((1,), (1,)))
        inv1 = inverse_factor(right[width:] - product(r01, r01, ((0,), (0,))))
        extra = pl.ds(rows, width)
        panels[col, extra] = jnp.where(first, inv0, inv1)
        panels[col, pl.ds(rows + width, width)] = r01
        for index in range(steps, steps + EXTRA):
            forward(col, index, panels.at[col])
            keep(col, index)

        @pl.loop(middle, steps)
        def _(index):
            take(second, index)
            add(second, index, panels.at[second])

        for index in range(steps, steps + EXTRA):
            take(second, index)

    @pl.when(jnp.logical_not(owner))
    def _():
        @pl.loop(0, steps + EXTRA + LAG)
        def _(step):
            @pl.when(step < steps + EXTRA)
            def _():
                take(main, step)

            @pl.when(step >= LAG)
            def _():
                take(second, step - LAG)

            @pl.when(step < steps)
            def _():
                add(main, step, panels.at[main])

            @pl.when(jnp.logical_and(step >= LAG, step < steps + LAG))
            def _():
                add(second, step - LAG, panels.at[second])

    sum_over_row(mixed, 1)
    sums_out[...] = total[1]

    for panel in range(PANELS):
        pltpu.make_async_copy(panels.at[panel], panels_out.at[panel], out_sem.at[panel]).wait()
        for child, (there, other) in enumerate(children(panel)):
            @pl.when(there)
            def _():
                pltpu.make_async_remote_copy(
                    src_ref=panels.at[panel],
                    dst_ref=panels.at[panel],
                    send_sem=send_sem.at[panel, child],
                    recv_sem=recv_sem.at[panel, 0],
                    device_id={"col": other},
                    device_id_type=MESH,
                ).wait_send()


def gather(matrix, n_row, n_x, n_z):
    rows, width = matrix.shape
    tile = width
    steps = rows // tile
    assert rows % (2 * tile) == 0
    deep, tall = PANELS * width, rows + EXTRA * width
    share = deep // n_row
    anywhere = pl.BlockSpec(memory_space=pl.ANY)
    return pl.pallas_call(
        functools.partial(gather_kernel, n_row, n_x, n_z, tile),
        out_shape=(
            jax.ShapeDtypeStruct((PANELS, tall, width), jnp.float32),
            jax.ShapeDtypeStruct((deep, width), jnp.float32),
        ),
        in_specs=[anywhere],
        out_specs=(anywhere, pl.BlockSpec(memory_space=pltpu.VMEM)),
        scratch_shapes=[
            pltpu.VMEM((PANELS, tall, width), jnp.float32),
            pltpu.VMEM((rows, width), jnp.float32),
            pltpu.VMEM((deep, width), jnp.float32),
            pltpu.VMEM((deep, width), jnp.float32),
            pltpu.VMEM((deep, width), jnp.float32),
            pltpu.VMEM((2, n_row - 1, share, width), jnp.float32),
            pltpu.VMEM((2, deep, width), jnp.float32),
            pltpu.SemaphoreType.DMA,
            pltpu.SemaphoreType.DMA((PANELS, steps + EXTRA)),
            pltpu.SemaphoreType.DMA((PANELS, 3)),
            pltpu.SemaphoreType.DMA((PANELS,)),
            pltpu.SemaphoreType.DMA((2, n_row - 1)),
            pltpu.SemaphoreType.DMA((2, n_row - 1)),
            pltpu.SemaphoreType.DMA((2, n_row - 1)),
            pltpu.SemaphoreType.DMA((2, n_row - 1)),
            pltpu.SemaphoreType.DMA((2,)),
        ],
        compiler_params=pltpu.CompilerParams(
            collective_id=0, has_side_effects=True, vmem_limit_bytes=60 * 1024 * 1024
        ),
    )(matrix)


def product(a, b, over=((1,), (0,))):
    return lax.dot_general(
        a, b, (over, ((), ())), precision=HIGHEST, preferred_element_type=jnp.float32
    )


def inverse_factor(gram):
    width = gram.shape[0]
    left, right = gram, eye(width)
    row_id = lax.broadcasted_iota(jnp.int32, (BLOCK, 1), 0)
    lane = lax.broadcasted_iota(jnp.int32, (BLOCK, width), 1)
    done = []
    for start in range(0, width, BLOCK):
        p, e = left[:BLOCK], right[:BLOCK]
        for s in range(BLOCK):
            column = p[:, start + s:start + s + 1]
            ratio = jnp.where(row_id > s, column / column[s:s + 1], 0.0)
            p, e = p - ratio * p[s:s + 1], e - ratio * e[s:s + 1]
        pivots = jnp.sum(jnp.where(lane == row_id + start, p, 0.0), axis=1, keepdims=True)
        scale = 1.0 / jnp.sqrt(pivots)
        p, e = p * scale, e * scale
        done.append(e)
        if start + BLOCK < width:
            change = outer(p, jnp.concatenate([p, e], axis=1))
            left = left[BLOCK:] - change[start + BLOCK:, :width]
            right = right[BLOCK:] - change[start + BLOCK:, width:]
    return jnp.concatenate(done, axis=0)


def eye(width):
    rows = lax.broadcasted_iota(jnp.int32, (width, width), 0)
    return jnp.where(rows == lax.broadcasted_iota(jnp.int32, (width, width), 1), 1.0, 0.0)


def coefficients(sums, inv0, r01, inv1, factor_scale, width, col):
    m0, m1 = sums[:width], sums[width:]
    scaled_eye = factor_scale * eye(width)
    down, turned = ((0,), (0,)), ((1,), (1,))
    cross0 = product(inv0, m0)
    n0 = jnp.where(col == 0, factor_scale * product(m0, inv0, turned), m0)
    n1 = jnp.where(col == 0, factor_scale * product(m1, inv0, turned), m1)
    cross1 = product(inv1, n1 - product(r01, product(inv0, n0), down))
    t1 = jnp.where(col == 1, -scaled_eye, jnp.where(col == 0, 0.0, cross1))
    t0 = jnp.where(col == 0, -scaled_eye, jnp.where(col == 1, 0.0, cross0))
    x1 = product(inv1, t1, down)
    x0 = product(inv0, t0 - product(r01, x1), down)
    return cross0, cross1, jnp.concatenate([x0, x1], axis=0)


def halves(a):
    high = a.astype(jnp.bfloat16)
    return high, (a - high.astype(jnp.float32)).astype(jnp.bfloat16)


def finish_kernel(
    factor_scale, tile, panels_ref, matrix_ref, sums_ref, r_ref, out_ref,
    panels, mine, factors, result, load_sem, out_sem,
):
    rows, width = mine.shape
    load_factors = pltpu.make_async_copy(
        panels_ref.at[:, pl.ds(rows, EXTRA * width)], factors, load_sem.at[2]
    )
    load_panels = pltpu.make_async_copy(
        panels_ref.at[:, pl.ds(0, rows)], panels, load_sem.at[0]
    )
    load_mine = pltpu.make_async_copy(matrix_ref, mine, load_sem.at[1])
    load_factors.start()
    load_panels.start()
    load_mine.start()
    col = lax.axis_index("col")
    load_factors.wait()
    inv0, r01, inv1 = factors[0, :width], factors[0, width:], factors[1, :width]
    cross0, cross1, mix = coefficients(
        sums_ref[...], inv0, r01, inv1, factor_scale, width, col
    )
    r_ref[0] = cross0 / factor_scale
    r_ref[1] = cross1 / factor_scale
    mix_high, mix_low = halves(mix)
    mix_both = jnp.concatenate([mix_high, mix_low], axis=1)
    load_panels.wait()
    load_mine.wait()
    keep = col >= PANELS

    @pl.loop(0, rows // tile)
    def _(index):
        at = pl.ds(pl.multiple_of(index * tile, tile), tile)
        high, low = halves(jnp.concatenate([panels[0, at], panels[1, at]], axis=1))
        main = jnp.dot(high, mix_both, preferred_element_type=jnp.float32)
        rest = jnp.dot(low, mix_high, preferred_element_type=jnp.float32)
        removed = main[:, :width] + (main[:, width:] + rest)
        result[at] = jnp.where(keep, mine[at], 0.0) - removed
        pltpu.make_async_copy(result.at[at], out_ref.at[at], out_sem).start()

    pltpu.make_async_copy(result, out_ref, out_sem).wait()


def finish(panels, matrix, sums, factor_scale):
    rows, width = matrix.shape
    anywhere = pl.BlockSpec(memory_space=pl.ANY)
    in_vmem = pl.BlockSpec(memory_space=pltpu.VMEM)
    return pl.pallas_call(
        functools.partial(finish_kernel, factor_scale, math.gcd(rows, 512)),
        out_shape=(
            jax.ShapeDtypeStruct((PANELS, width, width), jnp.float32),
            jax.ShapeDtypeStruct((rows, width), jnp.float32),
        ),
        in_specs=[anywhere, anywhere, in_vmem],
        out_specs=(in_vmem, anywhere),
        scratch_shapes=[
            pltpu.VMEM((PANELS, rows, width), jnp.float32),
            pltpu.VMEM((rows, width), jnp.float32),
            pltpu.VMEM((PANELS, EXTRA * width, width), jnp.float32),
            pltpu.VMEM((rows, width), jnp.float32),
            pltpu.SemaphoreType.DMA((3,)),
            pltpu.SemaphoreType.DMA,
        ],
        compiler_params=pltpu.CompilerParams(vmem_limit_bytes=60 * 1024 * 1024),
    )(panels, matrix, sums)


def solution(mesh):
    n_row, n_col = mesh.shape["row"], mesh.shape["col"]
    n_x = max(PANELS, n_row // 2)
    n_z = n_col // n_x
    assert n_x * n_z == n_col

    def local(matrix):
        rows, width = matrix.shape
        factor_scale = math.sqrt(rows * n_row)
        panels, sums = gather(matrix, n_row, n_x, n_z)
        return finish(panels, matrix, sums, factor_scale)

    return jax.shard_map(
        local,
        mesh=mesh,
        in_specs=(P("row", "col"),),
        out_specs=(P(None, None, "col"), P("row", "col")),
        check_vma=False,
    )
```

```python
import functools
import math

import jax
import jax.numpy as jnp
from jax import lax
from jax.experimental import pallas as pl
from jax.experimental.pallas import tpu as pltpu
from jax.sharding import PartitionSpec as P

MESH = pl.DeviceIdType.MESH
HIGHEST = lax.Precision.HIGHEST
PANELS = 2
LAG = 4
BLOCK = 32
EXTRA = 2
AHEAD = 6


def outer(a, b):
    return lax.dot_general(
        a, b, (((0,), (0,)), ((), ())), precision=HIGHEST, preferred_element_type=jnp.float32
    )


def gather_kernel(
    n_row, n_x, n_z, tile,
    matrix_ref, panels_out, sums_out,
    panels, mine, mixed, half, theirs, parts, total,
    mine_sem, recv_sem, send_sem, out_sem, scatter_send, scatter_recv, back_send, back_recv,
    swap_sem,
):
    rows, width = mine.shape
    steps = rows // tile
    row = lax.axis_index("row")
    col = lax.axis_index("col")
    x = lax.rem(col, n_x)
    z = col // n_x

    barrier = pltpu.get_barrier_semaphore()
    neighbours = (
        (x > 0, col - 1), (x < n_x - 1, col + 1), (z > 0, col - n_x), (z < n_z - 1, col + n_x)
    )
    for there, other in neighbours:
        @pl.when(there)
        def _():
            pl.semaphore_signal(barrier, inc=1, device_id={"col": other}, device_id_type=MESH)
    for step in range(1, n_row):
        peer = lax.rem(row + step, n_row)
        pl.semaphore_signal(barrier, inc=1, device_id={"row": peer}, device_id_type=MESH)
    load_mine = pltpu.make_async_copy(matrix_ref, mine, mine_sem)
    load_mine.start()
    mixed[...] = jnp.zeros_like(mixed)
    peers = n_row - 1
    for there, _ in neighbours:
        peers += jnp.where(there, 1, 0)
    pl.semaphore_wait(barrier, peers)

    def span(panel, index):
        turned = jnp.logical_and(panel == 1, index < steps)
        place = jnp.where(turned, steps - 1 - index, index)
        return pl.ds(pl.multiple_of(place * tile, tile), tile)

    def children(panel):
        return (
            (jnp.logical_and(x == panel, z < n_z - 1), col + n_x),
            (jnp.logical_and(x >= panel, x < n_x - 1), col + 1),
            (jnp.logical_and(x <= panel, x > 0), col - 1),
        )

    def forward(panel, index, source, which=(0, 1, 2)):
        for child, (there, other) in enumerate(children(panel)):
            if child not in which:
                continue

            @pl.when(there)
            def _():
                pltpu.make_async_remote_copy(
                    src_ref=source.at[span(panel, index)],
                    dst_ref=panels.at[panel, span(panel, index)],
                    send_sem=send_sem.at[panel, child],
                    recv_sem=recv_sem.at[panel, index],
                    device_id={"col": other},
                    device_id_type=MESH,
                ).start()

    def keep(panel, index):
        pltpu.make_async_copy(
            panels.at[panel, span(panel, index)],
            panels_out.at[panel, span(panel, index)],
            out_sem.at[panel],
        ).start()

    def take(panel, index):
        here = panels.at[panel, span(panel, index)]
        pltpu.make_async_copy(here, here, recv_sem.at[panel, index]).wait()
        forward(panel, index, panels.at[panel])
        keep(panel, index)

    def add(panel, index, source):
        at = span(panel, index)
        block = pl.ds(pl.multiple_of(panel * width, width), width)
        mixed[block] += outer(source[at], mine[at])

    share = mixed.shape[0] // n_row

    def part(index):
        return pl.ds(pl.multiple_of(index * share, share), share)

    def sum_over_row(source, turn):
        copies = []
        for step in range(1, n_row):
            peer = lax.rem(row + step, n_row)
            copies.append(pltpu.make_async_remote_copy(
                src_ref=source.at[part(peer)],
                dst_ref=parts.at[turn, step - 1],
                send_sem=scatter_send.at[turn, step - 1],
                recv_sem=scatter_recv.at[turn, step - 1],
                device_id={"row": peer},
                device_id_type=MESH,
            ))
            copies[-1].start()
        summed = source[part(row)]
        for step, copy in enumerate(copies):
            copy.wait_recv()
            summed += parts[turn, step]
        result = total.at[turn]
        result[part(row)] = summed
        backs = []
        for step in range(1, n_row):
            peer = lax.rem(row + step, n_row)
            backs.append(pltpu.make_async_remote_copy(
                src_ref=result.at[part(row)],
                dst_ref=result.at[part(row)],
                send_sem=back_send.at[turn, step - 1],
                recv_sem=back_recv.at[turn, step - 1],
                device_id={"row": peer},
                device_id_type=MESH,
            ))
            backs[-1].start()
        for copy in backs:
            copy.wait_recv()
        for copy in copies + backs:
            copy.wait_send()

    main = jnp.where(x == 1, 1, 0)
    second = 1 - main
    owner = col < PANELS
    middle = steps // 2

    @pl.when(owner)
    def _():
        @pl.loop(0, middle + AHEAD)
        def _(index):
            forward(col, index, matrix_ref)

        @pl.loop(middle + AHEAD, steps)
        def _(index):
            forward(col, index, matrix_ref, (0,))

        load_mine.wait()
        own = pltpu.make_async_copy(
            mine, panels_out.at[col, pl.ds(0, rows)], out_sem.at[col]
        )
        own.start()

        @pl.loop(0, steps)
        def _(index):
            add(col, index, mine)

        @pl.loop(0, middle)
        def _(index):
            take(second, index)
            add(second, index, panels.at[second])

        half[...] = mixed[...]
        sum_over_row(half, 0)
        swap = pltpu.make_async_remote_copy(
            src_ref=total.at[0],
            dst_ref=theirs,
            send_sem=swap_sem.at[0],
            recv_sem=swap_sem.at[1],
            device_id={"col": 1 - col},
            device_id_type=MESH,
        )
        swap.start()

        @pl.loop(middle + AHEAD, steps)
        def _(index):
            forward(col, index, matrix_ref, (1, 2))

        swap.wait()
        first = col == 0
        ours, other = total[0], theirs[...]
        left = jnp.where(first, ours, other)
        right = jnp.where(first, other, ours)
        inv0 = inverse_factor(left[:width])
        r01 = product(inv0, right[:width]) + product(inv0, left[width:], ((1,), (1,)))
        inv1 = inverse_factor(right[width:] - product(r01, r01, ((0,), (0,))))
        extra = pl.ds(rows, width)
        panels[col, extra] = jnp.where(first, inv0, inv1)
        corner = -product(product(inv1, r01, ((1,), (1,))), inv0)
        panels[col, pl.ds(rows + width, width)] = corner
        for index in range(steps, steps + EXTRA):
            forward(col, index, panels.at[col])
            keep(col, index)

        @pl.loop(middle, steps)
        def _(index):
            take(second, index)
            add(second, index, panels.at[second])

    @pl.when(jnp.logical_not(owner))
    def _():
        load_mine.wait()

        @pl.loop(0, steps + LAG)
        def _(step):
            @pl.when(step < steps + EXTRA)
            def _():
                take(main, step)

            @pl.when(step >= LAG)
            def _():
                take(second, step - LAG)

            @pl.when(step < steps)
            def _():
                add(main, step, panels.at[main])

            @pl.when(step >= LAG)
            def _():
                add(second, step - LAG, panels.at[second])

    sum_over_row(mixed, 1)
    sums_out[...] = total[1]
    for index in range(steps, steps + EXTRA):
        take(second, index)

    for panel in range(PANELS):
        pltpu.make_async_copy(panels.at[panel], panels_out.at[panel], out_sem.at[panel]).wait()
        for child, (there, other) in enumerate(children(panel)):
            @pl.when(there)
            def _():
                pltpu.make_async_remote_copy(
                    src_ref=panels.at[panel],
                    dst_ref=panels.at[panel],
                    send_sem=send_sem.at[panel, child],
                    recv_sem=recv_sem.at[panel, 0],
                    device_id={"col": other},
                    device_id_type=MESH,
                ).wait_send()


def gather(matrix, n_row, n_x, n_z):
    rows, width = matrix.shape
    tile = width
    steps = rows // tile
    assert rows % (2 * tile) == 0
    deep, tall = PANELS * width, rows + EXTRA * width
    share = deep // n_row
    anywhere = pl.BlockSpec(memory_space=pl.ANY)
    return pl.pallas_call(
        functools.partial(gather_kernel, n_row, n_x, n_z, tile),
        out_shape=(
            jax.ShapeDtypeStruct((PANELS, tall, width), jnp.float32),
            jax.ShapeDtypeStruct((deep, width), jnp.float32),
        ),
        in_specs=[anywhere],
        out_specs=(anywhere, pl.BlockSpec(memory_space=pltpu.VMEM)),
        scratch_shapes=[
            pltpu.VMEM((PANELS, tall, width), jnp.float32),
            pltpu.VMEM((rows, width), jnp.float32),
            pltpu.VMEM((deep, width), jnp.float32),
            pltpu.VMEM((deep, width), jnp.float32),
            pltpu.VMEM((deep, width), jnp.float32),
            pltpu.VMEM((2, n_row - 1, share, width), jnp.float32),
            pltpu.VMEM((2, deep, width), jnp.float32),
            pltpu.SemaphoreType.DMA,
            pltpu.SemaphoreType.DMA((PANELS, steps + EXTRA)),
            pltpu.SemaphoreType.DMA((PANELS, 3)),
            pltpu.SemaphoreType.DMA((PANELS,)),
            pltpu.SemaphoreType.DMA((2, n_row - 1)),
            pltpu.SemaphoreType.DMA((2, n_row - 1)),
            pltpu.SemaphoreType.DMA((2, n_row - 1)),
            pltpu.SemaphoreType.DMA((2, n_row - 1)),
            pltpu.SemaphoreType.DMA((2,)),
        ],
        compiler_params=pltpu.CompilerParams(
            collective_id=0, has_side_effects=True, vmem_limit_bytes=60 * 1024 * 1024
        ),
    )(matrix)


def product(a, b, over=((1,), (0,))):
    return lax.dot_general(
        a, b, (over, ((), ())), precision=HIGHEST, preferred_element_type=jnp.float32
    )


def inverse_factor(gram):
    width = gram.shape[0]
    left, right = gram, eye(width)
    row_id = lax.broadcasted_iota(jnp.int32, (BLOCK, 1), 0)
    lane = lax.broadcasted_iota(jnp.int32, (BLOCK, width), 1)
    done = []
    for start in range(0, width, BLOCK):
        p, e = left[:BLOCK], right[:BLOCK]
        for s in range(BLOCK):
            column = p[:, start + s:start + s + 1]
            ratio = jnp.where(row_id > s, column / column[s:s + 1], 0.0)
            p, e = p - ratio * p[s:s + 1], e - ratio * e[s:s + 1]
        pivots = jnp.sum(jnp.where(lane == row_id + start, p, 0.0), axis=1, keepdims=True)
        scale = 1.0 / jnp.sqrt(pivots)
        p, e = p * scale, e * scale
        done.append(e)
        if start + BLOCK < width:
            change = outer(p, jnp.concatenate([p, e], axis=1))
            left = left[BLOCK:] - change[start + BLOCK:, :width]
            right = right[BLOCK:] - change[start + BLOCK:, width:]
    return jnp.concatenate(done, axis=0)


def eye(width):
    rows = lax.broadcasted_iota(jnp.int32, (width, width), 0)
    return jnp.where(rows == lax.broadcasted_iota(jnp.int32, (width, width), 1), 1.0, 0.0)


def coefficients(sums, inv0, corner, inv1, factor_scale, width, col):
    scaled_eye = factor_scale * eye(width)
    down, turned = ((0,), (0,)), ((1,), (1,))
    cross0 = product(inv0, sums[:width])
    seen = jnp.where(col == 0, factor_scale * product(sums, inv0, turned), sums)
    cross1 = product(jnp.concatenate([corner, inv1], axis=1), seen)
    t1 = jnp.where(col == 1, -scaled_eye, jnp.where(col == 0, 0.0, cross1))
    t0 = jnp.where(col == 0, -scaled_eye, jnp.where(col == 1, 0.0, cross0))
    x1 = product(inv1, t1, down)
    x0 = product(inv0, t0, down) + product(corner, t1, down)
    return cross0, cross1, jnp.concatenate([x0, x1], axis=0)


def halves(a):
    high = a.astype(jnp.bfloat16)
    return high, (a - high.astype(jnp.float32)).astype(jnp.bfloat16)


def finish_kernel(
    factor_scale, tile, panels_ref, matrix_ref, sums_ref, r_ref, out_ref,
    panels, mine, factors, result, load_sem, out_sem,
):
    rows, width = mine.shape
    pieces = rows // tile
    load_factors = pltpu.make_async_copy(
        panels_ref.at[:, pl.ds(rows, EXTRA * width)], factors, load_sem.at[2, 0]
    )
    load_factors.start()

    def loads(index):
        at = pl.ds(pl.multiple_of(index * tile, tile), tile)
        return (
            pltpu.make_async_copy(panels_ref.at[:, at], panels.at[:, at], load_sem.at[0, index]),
            pltpu.make_async_copy(matrix_ref.at[at], mine.at[at], load_sem.at[1, index]),
        )

    @pl.loop(0, pieces)
    def _(index):
        for load in loads(index):
            load.start()

    col = lax.axis_index("col")
    load_factors.wait()
    inv0, corner, inv1 = factors[0, :width], factors[0, width:], factors[1, :width]
    cross0, cross1, mix = coefficients(
        sums_ref[...], inv0, corner, inv1, factor_scale, width, col
    )
    r_ref[0] = cross0 / factor_scale
    r_ref[1] = cross1 / factor_scale
    mix_high, mix_low = halves(mix)
    mix_both = jnp.concatenate([mix_high, mix_low], axis=1)
    keep = col >= PANELS

    @pl.loop(0, pieces)
    def _(index):
        for load in loads(index):
            load.wait()
        at = pl.ds(pl.multiple_of(index * tile, tile), tile)
        high, low = halves(jnp.concatenate([panels[0, at], panels[1, at]], axis=1))
        main = jnp.dot(high, mix_both, preferred_element_type=jnp.float32)
        rest = jnp.dot(low, mix_high, preferred_element_type=jnp.float32)
        removed = main[:, :width] + (main[:, width:] + rest)
        result[at] = jnp.where(keep, mine[at], 0.0) - removed
        pltpu.make_async_copy(result.at[at], out_ref.at[at], out_sem).start()

    pltpu.make_async_copy(result, out_ref, out_sem).wait()


def finish(panels, matrix, sums, factor_scale):
    rows, width = matrix.shape
    tile = math.gcd(rows, 1024)
    anywhere = pl.BlockSpec(memory_space=pl.ANY)
    in_vmem = pl.BlockSpec(memory_space=pltpu.VMEM)
    return pl.pallas_call(
        functools.partial(finish_kernel, factor_scale, tile),
        out_shape=(
            jax.ShapeDtypeStruct((PANELS, width, width), jnp.float32),
            jax.ShapeDtypeStruct((rows, width), jnp.float32),
        ),
        in_specs=[anywhere, anywhere, in_vmem],
        out_specs=(in_vmem, anywhere),
        scratch_shapes=[
            pltpu.VMEM((PANELS, rows, width), jnp.float32),
            pltpu.VMEM((rows, width), jnp.float32),
            pltpu.VMEM((PANELS, EXTRA * width, width), jnp.float32),
            pltpu.VMEM((rows, width), jnp.float32),
            pltpu.SemaphoreType.DMA((3, rows // tile)),
            pltpu.SemaphoreType.DMA,
        ],
        compiler_params=pltpu.CompilerParams(vmem_limit_bytes=60 * 1024 * 1024),
    )(panels, matrix, sums)


def solution(mesh):
    n_row, n_col = mesh.shape["row"], mesh.shape["col"]
    n_x = max(PANELS, n_row // 2)
    n_z = n_col // n_x
    assert n_x * n_z == n_col

    def local(matrix):
        rows, width = matrix.shape
        factor_scale = math.sqrt(rows * n_row)
        panels, sums = gather(matrix, n_row, n_x, n_z)
        return finish(panels, matrix, sums, factor_scale)

    return jax.shard_map(
        local,
        mesh=mesh,
        in_specs=(P("row", "col"),),
        out_specs=(P(None, None, "col"), P("row", "col")),
        check_vma=False,
    )
```

```python
import functools
import math

import jax
import jax.numpy as jnp
from jax import lax
from jax.experimental import pallas as pl
from jax.experimental.pallas import tpu as pltpu
from jax.sharding import PartitionSpec as P

MESH = pl.DeviceIdType.MESH
HIGHEST = lax.Precision.HIGHEST
PANELS = 2
LAG = 4
BLOCK = 32
EXTRA = 2
AHEAD = 6


def outer(a, b):
    return lax.dot_general(
        a, b, (((0,), (0,)), ((), ())), precision=HIGHEST, preferred_element_type=jnp.float32
    )


def gather_kernel(
    n_row, n_x, n_z, tile,
    matrix_ref, panels_out, sums_out,
    panels, mine, mixed, half, theirs, parts, total,
    mine_sem, recv_sem, send_sem, out_sem, scatter_send, scatter_recv, back_send, back_recv,
    swap_sem,
):
    rows, width = mine.shape
    steps = rows // tile
    row = lax.axis_index("row")
    col = lax.axis_index("col")
    x = lax.rem(col, n_x)
    z = col // n_x

    barrier = pltpu.get_barrier_semaphore()
    neighbours = (
        (x > 0, col - 1), (x < n_x - 1, col + 1), (z > 0, col - n_x), (z < n_z - 1, col + n_x)
    )
    for there, other in neighbours:
        @pl.when(there)
        def _():
            pl.semaphore_signal(barrier, inc=1, device_id={"col": other}, device_id_type=MESH)
    for step in range(1, n_row):
        peer = lax.rem(row + step, n_row)
        pl.semaphore_signal(barrier, inc=1, device_id={"row": peer}, device_id_type=MESH)
    load_mine = pltpu.make_async_copy(matrix_ref, mine, mine_sem)
    load_mine.start()
    mixed[...] = jnp.zeros_like(mixed)
    peers = n_row - 1
    for there, _ in neighbours:
        peers += jnp.where(there, 1, 0)
    pl.semaphore_wait(barrier, peers)

    def span(panel, index):
        turned = jnp.logical_and(panel == 1, index < steps)
        place = jnp.where(turned, steps - 1 - index, index)
        return pl.ds(pl.multiple_of(place * tile, tile), tile)

    def children(panel):
        return (
            (jnp.logical_and(x == panel, z < n_z - 1), col + n_x),
            (jnp.logical_and(x >= panel, x < n_x - 1), col + 1),
            (jnp.logical_and(x <= panel, x > 0), col - 1),
        )

    def forward(panel, index, source, which=(0, 1, 2)):
        for child, (there, other) in enumerate(children(panel)):
            if child not in which:
                continue

            @pl.when(there)
            def _():
                pltpu.make_async_remote_copy(
                    src_ref=source.at[span(panel, index)],
                    dst_ref=panels.at[panel, span(panel, index)],
                    send_sem=send_sem.at[panel, child],
                    recv_sem=recv_sem.at[panel, index],
                    device_id={"col": other},
                    device_id_type=MESH,
                ).start()

    def keep(panel, index):
        pltpu.make_async_copy(
            panels.at[panel, span(panel, index)],
            panels_out.at[panel, span(panel, index)],
            out_sem.at[panel],
        ).start()

    def take(panel, index):
        here = panels.at[panel, span(panel, index)]
        pltpu.make_async_copy(here, here, recv_sem.at[panel, index]).wait()
        forward(panel, index, panels.at[panel])
        keep(panel, index)

    def add(panel, index, source):
        at = span(panel, index)
        block = pl.ds(pl.multiple_of(panel * width, width), width)
        mixed[block] += outer(source[at], mine[at])

    share = mixed.shape[0] // n_row

    def part(index):
        return pl.ds(pl.multiple_of(index * share, share), share)

    def sum_over_row(source, turn):
        copies = []
        for step in range(1, n_row):
            peer = lax.rem(row + step, n_row)
            copies.append(pltpu.make_async_remote_copy(
                src_ref=source.at[part(peer)],
                dst_ref=parts.at[turn, step - 1],
                send_sem=scatter_send.at[turn, step - 1],
                recv_sem=scatter_recv.at[turn, step - 1],
                device_id={"row": peer},
                device_id_type=MESH,
            ))
            copies[-1].start()
        summed = source[part(row)]
        for step, copy in enumerate(copies):
            copy.wait_recv()
            summed += parts[turn, step]
        result = total.at[turn]
        result[part(row)] = summed
        backs = []
        for step in range(1, n_row):
            peer = lax.rem(row + step, n_row)
            backs.append(pltpu.make_async_remote_copy(
                src_ref=result.at[part(row)],
                dst_ref=result.at[part(row)],
                send_sem=back_send.at[turn, step - 1],
                recv_sem=back_recv.at[turn, step - 1],
                device_id={"row": peer},
                device_id_type=MESH,
            ))
            backs[-1].start()
        for copy in backs:
            copy.wait_recv()
        for copy in copies + backs:
            copy.wait_send()

    main = jnp.where(x == 1, 1, 0)
    second = 1 - main
    owner = col < PANELS
    middle = steps // 2

    @pl.when(owner)
    def _():
        @pl.loop(0, middle + AHEAD)
        def _(index):
            forward(col, index, matrix_ref)

        @pl.loop(middle + AHEAD, steps)
        def _(index):
            forward(col, index, matrix_ref, (0,))

        load_mine.wait()
        own = pltpu.make_async_copy(
            mine, panels_out.at[col, pl.ds(0, rows)], out_sem.at[col]
        )
        own.start()

        @pl.loop(0, steps)
        def _(index):
            add(col, index, mine)

        @pl.loop(0, middle)
        def _(index):
            take(second, index)
            add(second, index, panels.at[second])

        half[...] = mixed[...]
        sum_over_row(half, 0)
        swap = pltpu.make_async_remote_copy(
            src_ref=total.at[0],
            dst_ref=theirs,
            send_sem=swap_sem.at[0],
            recv_sem=swap_sem.at[1],
            device_id={"col": 1 - col},
            device_id_type=MESH,
        )
        swap.start()

        @pl.loop(middle + AHEAD, steps)
        def _(index):
            forward(col, index, matrix_ref, (1, 2))

        swap.wait()
        first = col == 0
        ours, other = total[0], theirs[...]
        left = jnp.where(first, ours, other)
        right = jnp.where(first, other, ours)
        inv0 = inverse_factor(left[:width])
        r01 = product(inv0, right[:width]) + product(inv0, left[width:], ((1,), (1,)))
        inv1 = inverse_factor(right[width:] - product(r01, r01, ((0,), (0,))))
        extra = pl.ds(rows, width)
        panels[col, extra] = jnp.where(first, inv0, inv1)
        corner = -product(product(inv1, r01, ((1,), (1,))), inv0)
        panels[col, pl.ds(rows + width, width)] = corner
        for index in range(steps, steps + EXTRA):
            forward(col, index, panels.at[col])
            keep(col, index)

        @pl.loop(middle, steps)
        def _(index):
            take(second, index)
            add(second, index, panels.at[second])

    @pl.when(jnp.logical_not(owner))
    def _():
        load_mine.wait()

        @pl.loop(0, steps + LAG)
        def _(step):
            @pl.when(step < steps + EXTRA)
            def _():
                take(main, step)

            @pl.when(step >= LAG)
            def _():
                take(second, step - LAG)

            @pl.when(step < steps)
            def _():
                add(main, step, panels.at[main])

            @pl.when(step >= LAG)
            def _():
                add(second, step - LAG, panels.at[second])

    sum_over_row(mixed, 1)
    sums_out[...] = total[1]
    for index in range(steps, steps + EXTRA):
        take(second, index)

    for panel in range(PANELS):
        pltpu.make_async_copy(panels.at[panel], panels_out.at[panel], out_sem.at[panel]).wait()
        for child, (there, other) in enumerate(children(panel)):
            @pl.when(there)
            def _():
                pltpu.make_async_remote_copy(
                    src_ref=panels.at[panel],
                    dst_ref=panels.at[panel],
                    send_sem=send_sem.at[panel, child],
                    recv_sem=recv_sem.at[panel, 0],
                    device_id={"col": other},
                    device_id_type=MESH,
                ).wait_send()


def gather(matrix, n_row, n_x, n_z):
    rows, width = matrix.shape
    tile = width
    steps = rows // tile
    assert rows % (2 * tile) == 0
    deep, tall = PANELS * width, rows + EXTRA * width
    share = deep // n_row
    anywhere = pl.BlockSpec(memory_space=pl.ANY)
    return pl.pallas_call(
        functools.partial(gather_kernel, n_row, n_x, n_z, tile),
        out_shape=(
            jax.ShapeDtypeStruct((PANELS, tall, width), jnp.float32),
            jax.ShapeDtypeStruct((deep, width), jnp.float32),
        ),
        in_specs=[anywhere],
        out_specs=(anywhere, pl.BlockSpec(memory_space=pltpu.VMEM)),
        scratch_shapes=[
            pltpu.VMEM((PANELS, tall, width), jnp.float32),
            pltpu.VMEM((rows, width), jnp.float32),
            pltpu.VMEM((deep, width), jnp.float32),
            pltpu.VMEM((deep, width), jnp.float32),
            pltpu.VMEM((deep, width), jnp.float32),
            pltpu.VMEM((2, n_row - 1, share, width), jnp.float32),
            pltpu.VMEM((2, deep, width), jnp.float32),
            pltpu.SemaphoreType.DMA,
            pltpu.SemaphoreType.DMA((PANELS, steps + EXTRA)),
            pltpu.SemaphoreType.DMA((PANELS, 3)),
            pltpu.SemaphoreType.DMA((PANELS,)),
            pltpu.SemaphoreType.DMA((2, n_row - 1)),
            pltpu.SemaphoreType.DMA((2, n_row - 1)),
            pltpu.SemaphoreType.DMA((2, n_row - 1)),
            pltpu.SemaphoreType.DMA((2, n_row - 1)),
            pltpu.SemaphoreType.DMA((2,)),
        ],
        compiler_params=pltpu.CompilerParams(
            collective_id=0, has_side_effects=True, vmem_limit_bytes=60 * 1024 * 1024
        ),
    )(matrix)


def product(a, b, over=((1,), (0,))):
    return lax.dot_general(
        a, b, (over, ((), ())), precision=HIGHEST, preferred_element_type=jnp.float32
    )


def inverse_factor(gram):
    width = gram.shape[0]
    left, right = gram, eye(width)
    row_id = lax.broadcasted_iota(jnp.int32, (BLOCK, 1), 0)
    lane = lax.broadcasted_iota(jnp.int32, (BLOCK, width), 1)
    done = []
    for start in range(0, width, BLOCK):
        p, e = left[:BLOCK], right[:BLOCK]
        for s in range(BLOCK):
            column = p[:, start + s:start + s + 1]
            ratio = jnp.where(row_id > s, column / column[s:s + 1], 0.0)
            p, e = p - ratio * p[s:s + 1], e - ratio * e[s:s + 1]
        pivots = jnp.sum(jnp.where(lane == row_id + start, p, 0.0), axis=1, keepdims=True)
        scale = 1.0 / jnp.sqrt(pivots)
        p, e = p * scale, e * scale
        done.append(e)
        if start + BLOCK < width:
            change = outer(p, jnp.concatenate([p, e], axis=1))
            left = left[BLOCK:] - change[start + BLOCK:, :width]
            right = right[BLOCK:] - change[start + BLOCK:, width:]
    return jnp.concatenate(done, axis=0)


def eye(width):
    rows = lax.broadcasted_iota(jnp.int32, (width, width), 0)
    return jnp.where(rows == lax.broadcasted_iota(jnp.int32, (width, width), 1), 1.0, 0.0)


def coefficients(sums, inv0, corner, inv1, factor_scale, width, col):
    scaled_eye = factor_scale * eye(width)
    down, turned = ((0,), (0,)), ((1,), (1,))
    cross0 = product(inv0, sums[:width])
    seen = jnp.where(col == 0, factor_scale * product(sums, inv0, turned), sums)
    cross1 = product(jnp.concatenate([corner, inv1], axis=1), seen)
    t1 = jnp.where(col == 1, -scaled_eye, jnp.where(col == 0, 0.0, cross1))
    t0 = jnp.where(col == 0, -scaled_eye, jnp.where(col == 1, 0.0, cross0))
    x1 = product(inv1, t1, down)
    x0 = product(inv0, t0, down) + product(corner, t1, down)
    return cross0, cross1, jnp.concatenate([x0, x1], axis=0)


def halves(a):
    high = a.astype(jnp.bfloat16)
    return high, (a - high.astype(jnp.float32)).astype(jnp.bfloat16)


def finish_kernel(
    factor_scale, tile, panels_ref, matrix_ref, sums_ref, r_ref, out_ref,
    panels, mine, factors, result, load_sem, out_sem,
):
    rows, width = mine.shape
    pieces = rows // tile
    load_factors = pltpu.make_async_copy(
        panels_ref.at[:, pl.ds(rows, EXTRA * width)], factors, load_sem.at[2, 0]
    )
    load_factors.start()

    def loads(index):
        at = pl.ds(pl.multiple_of(index * tile, tile), tile)
        return (
            pltpu.make_async_copy(panels_ref.at[:, at], panels.at[:, at], load_sem.at[0, index]),
            pltpu.make_async_copy(matrix_ref.at[at], mine.at[at], load_sem.at[1, index]),
        )

    @pl.loop(0, pieces)
    def _(index):
        for load in loads(index):
            load.start()

    col = lax.axis_index("col")
    load_factors.wait()
    inv0, corner, inv1 = factors[0, :width], factors[0, width:], factors[1, :width]
    cross0, cross1, mix = coefficients(
        sums_ref[...], inv0, corner, inv1, factor_scale, width, col
    )
    r_ref[0] = cross0 / factor_scale
    r_ref[1] = cross1 / factor_scale
    mix_high, mix_low = halves(mix)
    mix_both = jnp.concatenate([mix_high, mix_low], axis=1)
    keep = col >= PANELS

    @pl.loop(0, pieces)
    def _(index):
        for load in loads(index):
            load.wait()
        at = pl.ds(pl.multiple_of(index * tile, tile), tile)
        high, low = halves(jnp.concatenate([panels[0, at], panels[1, at]], axis=1))
        main = jnp.dot(high, mix_both, preferred_element_type=jnp.float32)
        rest = jnp.dot(low, mix_high, preferred_element_type=jnp.float32)
        removed = main[:, :width] + (main[:, width:] + rest)
        result[at] = jnp.where(keep, mine[at], 0.0) - removed
        pltpu.make_async_copy(result.at[at], out_ref.at[at], out_sem).start()

    pltpu.make_async_copy(result, out_ref, out_sem).wait()


def finish(panels, matrix, sums, factor_scale):
    rows, width = matrix.shape
    tile = math.gcd(rows, 512)
    anywhere = pl.BlockSpec(memory_space=pl.ANY)
    in_vmem = pl.BlockSpec(memory_space=pltpu.VMEM)
    return pl.pallas_call(
        functools.partial(finish_kernel, factor_scale, tile),
        out_shape=(
            jax.ShapeDtypeStruct((PANELS, width, width), jnp.float32),
            jax.ShapeDtypeStruct((rows, width), jnp.float32),
        ),
        in_specs=[anywhere, anywhere, in_vmem],
        out_specs=(in_vmem, anywhere),
        scratch_shapes=[
            pltpu.VMEM((PANELS, rows, width), jnp.float32),
            pltpu.VMEM((rows, width), jnp.float32),
            pltpu.VMEM((PANELS, EXTRA * width, width), jnp.float32),
            pltpu.VMEM((rows, width), jnp.float32),
            pltpu.SemaphoreType.DMA((3, rows // tile)),
            pltpu.SemaphoreType.DMA,
        ],
        compiler_params=pltpu.CompilerParams(vmem_limit_bytes=60 * 1024 * 1024),
    )(panels, matrix, sums)


def solution(mesh):
    n_row, n_col = mesh.shape["row"], mesh.shape["col"]
    n_x = max(PANELS, n_row // 2)
    n_z = n_col // n_x
    assert n_x * n_z == n_col

    def local(matrix):
        rows, width = matrix.shape
        factor_scale = math.sqrt(rows * n_row)
        panels, sums = gather(matrix, n_row, n_x, n_z)
        return finish(panels, matrix, sums, factor_scale)

    return jax.shard_map(
        local,
        mesh=mesh,
        in_specs=(P("row", "col"),),
        out_specs=(P(None, None, "col"), P("row", "col")),
        check_vma=False,
    )
```
